128 devices in a mesh: wide: 16 (over x, y_hi, core), narrow: 8 (over z, y_lo).
Axes of the slice: x: 4, y: 4 (y_hi: 2, y_lo: 2; y = y_hi * 2 + y_lo), z: 4, core: 2. Of those that a mesh axis runs over, the one named last changes fastest.
Arguments:
- dosages: int32 [2048, 24576], P('narrow', 'wide'), may hold values from 0 to 3, as said below
- allele_counts: int32 [2048], P('narrow'), may hold values from 4000 to 384000, as said below
- called_counts: int32 [2048], P('narrow'), may hold values from 200000 to 400000
Outputs:
- relation: float32 [16, 8, 192, 24576], P(None, 'narrow', None, 'wide')
The draws below stay inside these ranges and needn't reach their ends.
Inputs may be any that keep to these rules, and one draw needn't show every extreme that they name: 3 marks a missing call; 0, 1 and 2 are dosages. `allele_counts`: the floor of the SNP's called_counts times a whole number p from 1 to 48, divided by 50, so that freq lies in (0, 0.5).
All inputs are finite; a program needn't handle non-finite values.
Results may differ from the reference program's by a relative error of at most 0.0043.
Values may be sent and summed in bfloat16 or wider, within the bound.
A program may use at most 128 MiB of HBM per device.

```python
import jax
import jax.numpy as jnp
from jax import lax

SNPS = 2048
SUB = 192
COHORT = 400000
BLK = 1536
SAMPLES = 24576
N_WIDE = 16
N_NARROW = 8


def cohort_counts(key):
    called_counts = jax.random.randint(jax.random.fold_in(key, 11), (SNPS,), COHORT // 2, COHORT + 1)
    percent = jax.random.randint(jax.random.fold_in(key, 12), (SNPS,), 1, 49)
    called_counts = called_counts.at[0].set(COHORT).at[1].set(COHORT // 2)
    percent = percent.at[0].set(48).at[1].set(1)
    allele_counts = called_counts * percent // 50
    return (called_counts, allele_counts)


def draw_allele_counts(key, part):
    return cohort_counts(key)[1].astype(jnp.int32)


def draw_called_counts(key, part):
    return cohort_counts(key)[0].astype(jnp.int32)


def draw_dosages(key, part):
    called_counts, allele_counts = cohort_counts(key)
    copies_top = (2 * called_counts)[:, None]
    first = jax.random.randint(jax.random.fold_in(key, 21), (SNPS, SAMPLES), 0, copies_top)
    second = jax.random.randint(jax.random.fold_in(key, 22), (SNPS, SAMPLES), 0, copies_top)
    dosage = (first < allele_counts[:, None]).astype(jnp.int32) + (second < allele_counts[:, None]).astype(jnp.int32)
    missing = jax.random.randint(jax.random.fold_in(key, 23), (SNPS, SAMPLES), 0, 20) == 0
    return jnp.where(missing, 3, dosage).astype(jnp.int32)


def setup_inputs(seed: int = 0) -> dict:
    arg_keys = jax.random.split(jax.random.key(seed), 4)
    return {
        "dosages": draw_dosages(jax.random.fold_in(arg_keys[3], 71), 0),
        "allele_counts": draw_allele_counts(jax.random.fold_in(arg_keys[3], 71), 0),
        "called_counts": draw_called_counts(jax.random.fold_in(arg_keys[3], 71), 0),
    }


def standardize(dosages, allele_counts, called_counts):
    freq = allele_counts.astype(jnp.float32) / (2.0 * called_counts.astype(jnp.float32))
    freq = freq[:, None]
    values = (dosages.astype(jnp.float32) - 2.0 * freq) * lax.rsqrt(2.0 * freq * (1.0 - freq))
    values = jnp.where(dosages == 3, jnp.zeros_like(values), values)
    return values.astype(jnp.bfloat16)

def reference(dosages, allele_counts, called_counts):
    standard = standardize(dosages, allele_counts, called_counts)
    blocks = jnp.transpose(standard.reshape(SNPS, N_WIDE, BLK), (1, 0, 2))

    def row_block(piece):
        product = lax.dot_general(piece, standard, (((0,), (0,)), ((), ())), preferred_element_type=jnp.float32)
        return product / SNPS
    grm = lax.map(row_block, blocks)
    return grm.reshape(N_WIDE, N_NARROW, SUB, SAMPLES)
```

```python
import functools

import jax
import jax.numpy as jnp
from jax import lax
from jax.experimental import pallas as pl
from jax.experimental.pallas import tpu as pltpu
from jax.sharding import PartitionSpec as P

MESH = pl.DeviceIdType.MESH
SNPS = 2048
SUB = 192
NARROW = 8
WIDE = 16
PIECE = SNPS // NARROW
CHUNK = 2 * PIECE
STEPS = (0, 1, 3, 2)
PEERS = ((0, 1), (1, 0), (3, 0), (1, 1), (3, 1), (2, 0), (2, 1))


def standardize(dosages, allele_counts, called_counts):
    freq = allele_counts.astype(jnp.float32) / (2.0 * called_counts.astype(jnp.float32))
    freq = freq[:, None]
    values = (dosages.astype(jnp.float32) - 2.0 * freq) * lax.rsqrt(2.0 * freq * (1.0 - freq))
    values = jnp.where(dosages == 3, jnp.zeros_like(values), values)
    return values.astype(jnp.bfloat16)


def gather_kernel(own_ref, wide_ref, narrow_ref, a2a_send, a2a_recv, local_sem, far_send, far_recv, sib_send, sib_recv, near_send, near_recv):
    w, n = lax.axis_index("wide"), lax.axis_index("narrow")
    x, yh, c = w // 4, (w // 2) % 2, w % 2
    z, yl = n // 2, n % 2

    def wide_id(dx, flip, core):
        return ((x + dx) % 4) * 4 + (1 - yh if flip else yh) * 2 + (1 - c if core else c)

    def narrow_id(dz, flip):
        return ((z + dz) % 4) * 2 + (1 - yl if flip else yl)

    def at_wide(dx, flip, core):
        return {"wide": wide_id(dx, flip, core), "narrow": n}

    def at_narrow(dz, flip):
        return {"wide": w, "narrow": narrow_id(dz, flip)}

    targets = [at_narrow(*p) for p in PEERS]
    targets += [at_wide(1, 0, 0), at_wide(3, 0, 0), at_wide(0, 1, 0), at_wide(0, 0, 1)]
    barrier = pltpu.get_barrier_semaphore()
    for t in targets:
        pl.semaphore_signal(barrier, inc=1, device_id=t, device_id_type=MESH)
    pl.semaphore_wait(barrier, len(targets))

    def lanes(start, size):
        return pl.ds(pl.multiple_of(start, size), size)

    def piece(ref, slot, k):
        return ref.at[slot, :, lanes(k * PIECE, PIECE)]

    def chunk(ref, slot, k):
        return ref.at[slot, :, lanes(k * CHUNK, CHUNK)]

    sent = []

    def send(src, dst, ssem, rsem, device):
        copy = pltpu.make_async_remote_copy(
            src_ref=src, dst_ref=dst, send_sem=ssem, recv_sem=rsem, device_id=device, device_id_type=MESH
        )
        copy.start()
        sent.append(copy)

    def arrive(ref, ssem, rsem, device):
        pltpu.make_async_remote_copy(
            src_ref=ref, dst_ref=ref, send_sem=ssem, recv_sem=rsem, device_id=device, device_id_type=MESH
        ).wait_recv()

    for i, (dz, flip) in enumerate(PEERS):
        send(own_ref.at[narrow_id(dz, flip)], piece(wide_ref, w, n), a2a_send.at[i], a2a_recv.at[i], at_narrow(dz, flip))
    own_copy = pltpu.make_async_copy(own_ref.at[n], piece(wide_ref, w, n), local_sem.at[4])
    own_copy.start()

    def wide_far(dx, flip, k, way, device):
        slot = wide_id(dx, flip, 0)
        ref = chunk(wide_ref, slot, (z + STEPS[k]) % 4)
        send(ref, ref, far_send.at[way, k], far_recv.at[way, k], device)

    def wide_sib(dx, flip, k, way):
        slot = wide_id(dx, flip, 0)
        ref = chunk(wide_ref, slot, (z + STEPS[k]) % 4)
        send(ref, ref, sib_send.at[way, k], sib_recv.at[way, k], at_wide(0, 0, 1))

    def wide_arrive(dx, flip, k, way):
        ref = chunk(wide_ref, wide_id(dx, flip, 0), (z + STEPS[k]) % 4)
        arrive(ref, far_send.at[way, k], far_recv.at[way, k], at_wide(0, 1, 0))

    def near_far(dz, flip, k, way, device):
        ref = chunk(narrow_ref, narrow_id(dz, flip), (z + dz + STEPS[k]) % 4)
        send(ref, ref, near_send.at[way, k], near_recv.at[way, k], device)

    def near_arrive(dz, flip, k, way):
        ref = chunk(narrow_ref, narrow_id(dz, flip), (z + dz + STEPS[k]) % 4)
        arrive(ref, near_send.at[way, k], near_recv.at[way, k], at_narrow(0, 1))

    xp, xm, yhp = at_wide(1, 0, 0), at_wide(3, 0, 0), at_wide(0, 1, 0)
    zp, zm, ylp = at_narrow(1, 0), at_narrow(3, 0), at_narrow(0, 1)
    local = []

    def own_chunk(k):
        d = STEPS[k]
        if k == 0:
            own_copy.wait()
        for i, (dz, flip) in enumerate(PEERS):
            if (4 - dz) % 4 == d:
                arrive(piece(wide_ref, w, narrow_id(d, flip)), a2a_send.at[i], a2a_recv.at[i], ylp)
        wide_far(0, 0, k, 0, xp)
        wide_far(0, 0, k, 1, xm)
        wide_far(0, 0, k, 2, yhp)
        src = chunk(wide_ref, w, (z + d) % 4)
        dst = chunk(narrow_ref, n, (z + d) % 4)
        send(src, dst, near_send.at[0, k], near_recv.at[0, k], zp)
        send(src, dst, near_send.at[1, k], near_recv.at[1, k], zm)
        send(src, dst, near_send.at[2, k], near_recv.at[2, k], ylp)
        wide_sib(0, 0, k, 0)
        copy = pltpu.make_async_copy(src, dst, local_sem.at[k])
        copy.start()
        local.append(copy)

    def neighbours(k):
        wide_arrive(3, 0, k, 0)
        if k < 2:
            wide_far(3, 0, k, 3, xp)
        wide_sib(3, 0, k, 1)
        near_arrive(3, 0, k, 0)
        if k < 2:
            near_far(3, 0, k, 3, zp)
        wide_arrive(1, 0, k, 1)
        if k >= 2:
            wide_far(1, 0, k, 3, xm)
        wide_sib(1, 0, k, 2)
        near_arrive(1, 0, k, 1)
        if k >= 2:
            near_far(1, 0, k, 3, zm)

    def partners(k):
        wide_arrive(0, 1, k, 2)
        wide_far(0, 1, k, 4, xp)
        wide_far(0, 1, k, 5, xm)
        wide_sib(0, 1, k, 3)
        near_arrive(0, 1, k, 2)
        near_far(0, 1, k, 4, zp)
        near_far(0, 1, k, 5, zm)

    def partner_neighbours(k):
        wide_arrive(3, 1, k, 4)
        if k < 2:
            wide_far(3, 1, k, 6, xp)
        wide_sib(3, 1, k, 4)
        near_arrive(3, 1, k, 4)
        if k < 2:
            near_far(3, 1, k, 6, zp)
        wide_arrive(1, 1, k, 5)
        if k >= 2:
            wide_far(1, 1, k, 6, xm)
        wide_sib(1, 1, k, 5)
        near_arrive(1, 1, k, 5)
        if k >= 2:
            near_far(1, 1, k, 6, zm)

    def opposite(k, flip):
        way = 6 if flip else 3
        wide_arrive(2, flip, k, way)
        wide_sib(2, flip, k, 6 + flip)
        near_arrive(2, flip, k, way)

    for k in range(4):
        own_chunk(k)
    neighbours(0)
    neighbours(1)
    partners(0)
    neighbours(2)
    partners(1)
    neighbours(3)
    opposite(0, 0)
    opposite(2, 0)
    partners(2)
    opposite(1, 0)
    opposite(3, 0)
    partners(3)
    for k in range(4):
        partner_neighbours(k)
    for k in (0, 2, 1, 3):
        opposite(k, 1)
    order = ((0, 0), (3, 0), (1, 0), (0, 1), (3, 1), (1, 1), (2, 0), (2, 1))
    for way, (dx, flip) in enumerate(order):
        for k in range(4):
            ref = chunk(wide_ref, wide_id(dx, flip, 1), (z + STEPS[k]) % 4)
            arrive(ref, sib_send.at[way, k], sib_recv.at[way, k], at_wide(0, 0, 1))
    for copy in local:
        copy.wait()
    for copy in sent:
        copy.wait_send()


def gather(own, space):
    dma = pltpu.SemaphoreType.DMA
    return pl.pallas_call(
        gather_kernel,
        out_shape=(
            jax.ShapeDtypeStruct((WIDE, SUB, SNPS), jnp.bfloat16),
            jax.ShapeDtypeStruct((NARROW, SUB, SNPS), jnp.bfloat16),
        ),
        in_specs=[pl.BlockSpec(memory_space=pltpu.VMEM)],
        out_specs=(pl.BlockSpec(memory_space=space), pl.BlockSpec(memory_space=space)),
        scratch_shapes=[
            dma((7,)), dma((7,)), dma((5,)),
            dma((7, 4)), dma((7, 4)), dma((8, 4)), dma((8, 4)), dma((7, 4)), dma((7, 4)),
        ],
        compiler_params=pltpu.CompilerParams(collective_id=0, has_side_effects=True, vmem_limit_bytes=48 * 1024 * 1024),
    )(own)


def shards(dosages, allele_counts, called_counts):
    standard = standardize(dosages, allele_counts, called_counts)
    own = standard.T.reshape(NARROW, SUB, PIECE)
    wide, narrow = gather(own, pl.ANY)
    rows, cols = wide.reshape(WIDE * SUB, SNPS), narrow.reshape(NARROW * SUB, SNPS)
    result = lax.dot_general(rows, cols, (((1,), (1,)), ((), ())), preferred_element_type=jnp.float32) / SNPS
    return result.reshape(WIDE, 1, SUB, NARROW * SUB)


def solution(mesh):
    return jax.shard_map(
        shards,
        mesh=mesh,
        in_specs=(P("narrow", "wide"), P("narrow"), P("narrow")),
        out_specs=P(None, "narrow", None, "wide"),
        check_vma=False,
    )
```

```python
import jax
import jax.numpy as jnp
from jax import lax
from jax.experimental import pallas as pl
from jax.experimental.pallas import tpu as pltpu
from jax.sharding import PartitionSpec as P

MESH = pl.DeviceIdType.MESH
SNPS = 2048
SUB = 192
NARROW = 8
WIDE = 16
BLK = NARROW * SUB
PIECE = SNPS // NARROW
QUARTER = SNPS // 4
ROWS = 2 * SUB
COLS = 4 * SUB
NEAR, OPPOSITE, FAR = 2, 4, 6


def standardize(dosages, allele_counts, called_counts):
    freq = allele_counts.astype(jnp.float32) / (2.0 * called_counts.astype(jnp.float32))
    freq = freq[:, None]
    values = (dosages.astype(jnp.float32) - 2.0 * freq) * lax.rsqrt(2.0 * freq * (1.0 - freq))
    values = jnp.where(dosages == 3, jnp.zeros_like(values), values)
    return values.astype(jnp.bfloat16)


def quarter_start(z, yl, q):
    half = z // 2
    return (yl if q < 2 else 1 - yl) * (SNPS // 2) + (half if q % 2 == 0 else 1 - half) * QUARTER


def tile(wide_ref, narrow_ref, start, i, j):
    lanes = pl.ds(pl.multiple_of(start, QUARTER), QUARTER)
    rows = wide_ref[pl.ds(2 * i, 2), :, lanes].reshape(ROWS, QUARTER)
    cols = narrow_ref[pl.ds(4 * j, 4), :, lanes].reshape(COLS, QUARTER)
    return lax.dot_general(rows, cols, (((1,), (1,)), ((), ())), preferred_element_type=jnp.float32)


def spot(i, j):
    return pl.ds(pl.multiple_of(i * ROWS, ROWS), ROWS), pl.ds(pl.multiple_of(j * COLS, COLS), COLS)


def gather_kernel(
    own_ref, wide_ref, narrow_ref, sum_ref,
    a2a_send, a2a_recv, local_sem, far_send, far_recv, sib_send, sib_recv, near_send, near_recv,
):
    w, n = lax.axis_index("wide"), lax.axis_index("narrow")
    x, yh, c = w // 4, (w // 2) % 2, w % 2
    z, yl = n // 2, n % 2

    def wide_id(dx, flip, core):
        return ((x + dx) % 4) * 4 + (1 - yh if flip else yh) * 2 + (1 - c if core else c)

    def ring(a):
        return (z, z + 1 - 2 * (z % 2), (z + 2) % 4, 3 - z)[a]

    def side(b):
        return 1 - yl if b else yl

    def narrow_id(label):
        return 2 * ring(label // 2) + side(label % 2)

    def at_wide(dx, flip, core):
        return {"wide": wide_id(dx, flip, core), "narrow": n}

    def at_narrow(label):
        return {"wide": w, "narrow": narrow_id(label)}

    xp, xm, yhp, sib = at_wide(1, 0, 0), at_wide(3, 0, 0), at_wide(0, 1, 0), at_wide(0, 0, 1)
    targets = [at_narrow(label) for label in range(1, NARROW)] + [xp, xm, yhp, sib]
    barrier = pltpu.get_barrier_semaphore()
    for t in targets:
        pl.semaphore_signal(barrier, inc=1, device_id=t, device_id_type=MESH)
    pl.semaphore_wait(barrier, len(targets))

    def slice_lanes(label):
        start = side(label % 2) * (SNPS // 2) + ring(label // 2) * PIECE
        return pl.ds(pl.multiple_of(start, PIECE), PIECE)

    def quarter_lanes(q, half=None):
        start = quarter_start(z, yl, q)
        if half is None:
            return pl.ds(pl.multiple_of(start, QUARTER), QUARTER)
        return pl.ds(pl.multiple_of(start + half * PIECE, PIECE), PIECE)

    sent = []

    def send(src, dst, ssem, rsem, device, keep=True):
        copy = pltpu.make_async_remote_copy(
            src_ref=src, dst_ref=dst, send_sem=ssem, recv_sem=rsem, device_id=device, device_id_type=MESH
        )
        copy.start()
        if keep:
            sent.append(copy)

    def described(ref, ssem, rsem, device):
        return pltpu.make_async_remote_copy(
            src_ref=ref, dst_ref=ref, send_sem=ssem, recv_sem=rsem, device_id=device, device_id_type=MESH
        )

    for label in (NEAR, FAR, OPPOSITE, 1, NEAR + 1, FAR + 1, OPPOSITE + 1):
        send(
            own_ref.at[narrow_id(label)], wide_ref.at[w, :, slice_lanes(0)],
            a2a_send.at[label - 1], a2a_recv.at[label - 1], at_narrow(label),
        )
    own_piece = pltpu.make_async_copy(own_ref.at[n], wide_ref.at[w, :, slice_lanes(0)], local_sem.at[4])
    own_piece.start()
    own_slice = pltpu.make_async_copy(own_ref, narrow_ref.at[:, :, slice_lanes(0)], local_sem.at[5])
    own_slice.start()
    local = [own_slice]
    groups = []

    def near_send_group(source, receiver, labels, sem):
        for i in labels:
            piece = receiver ^ i
            k = narrow_id(piece)
            lanes = slice_lanes(source)
            if source == 0:
                src = own_ref.at[k]
            elif piece == 0:
                src = wide_ref.at[w, :, lanes]
            else:
                src = narrow_ref.at[k, :, lanes]
            send(src, narrow_ref.at[k, :, lanes], near_send.at[sem], near_recv.at[sem], at_narrow(receiver), keep=False)
        groups.append((len(labels), source, sem, receiver))

    def near_arrive(count, source, sem):
        ref = narrow_ref.at[pl.ds(0, count), :, slice_lanes(source)]
        described(ref, near_send.at[sem], near_recv.at[sem], at_narrow(1)).wait_recv()

    def wide_send(dx, flip, q, sem, device, half=None):
        ref = wide_ref.at[wide_id(dx, flip, 0), :, quarter_lanes(q, half)]
        send(ref, ref, far_send.at[sem, q], far_recv.at[sem, q], device)

    def wide_arrive(dx, flip, q, sem, half=None):
        ref = wide_ref.at[wide_id(dx, flip, 0), :, quarter_lanes(q, half)]
        described(ref, far_send.at[sem, q], far_recv.at[sem, q], yhp).wait_recv()

    def share(dx, flip, q, sem):
        ref = wide_ref.at[wide_id(dx, flip, 0), :, quarter_lanes(q)]
        send(ref, ref, sib_send.at[sem, q], sib_recv.at[sem, q], sib)

    def own(q):
        labels = ((NEAR,), (FAR, OPPOSITE), (1, NEAR + 1), (FAR + 1, OPPOSITE + 1))[q]
        if q == 0:
            own_piece.wait()
        for label in labels:
            ref = wide_ref.at[w, :, slice_lanes(label)]
            described(ref, a2a_send.at[label - 1], a2a_recv.at[label - 1], at_narrow(1)).wait_recv()
        wide_send(0, 0, q, 0, xp)
        wide_send(0, 0, q, 1, xm)
        wide_send(0, 0, q, 2, yhp)
        share(0, 0, q, 0)
        lanes = slice_lanes(NEAR) if q == 0 else quarter_lanes(q)
        copy = pltpu.make_async_copy(wide_ref.at[w, :, lanes], narrow_ref.at[n, :, lanes], local_sem.at[q])
        copy.start()
        local.append(copy)

    def neighbours(q):
        wide_arrive(3, 0, q, 0)
        wide_send(3, 0, q, 5, xp, half=0)
        share(3, 0, q, 1)
        wide_arrive(1, 0, q, 1)
        wide_send(1, 0, q, 6, xm, half=1)
        share(1, 0, q, 2)

    def opposite(q):
        wide_arrive(2, 0, q, 5, half=0)
        wide_arrive(2, 0, q, 6, half=1)
        share(2, 0, q, 3)

    def partner(q):
        wide_arrive(0, 1, q, 2)
        wide_send(0, 1, q, 3, xp)
        wide_send(0, 1, q, 4, xm)
        share(0, 1, q, 4)

    def partner_neighbours(q):
        wide_arrive(3, 1, q, 3)
        wide_send(3, 1, q, 7, xp, half=0)
        share(3, 1, q, 5)
        wide_arrive(1, 1, q, 4)
        wide_send(1, 1, q, 8, xm, half=1)
        share(1, 1, q, 6)

    def partner_opposite(q):
        wide_arrive(2, 1, q, 7, half=0)
        wide_arrive(2, 1, q, 8, half=1)
        share(2, 1, q, 7)

    def shared(q):
        order = ((0, 0), (3, 0), (1, 0), (2, 0), (0, 1), (3, 1), (1, 1), (2, 1))
        for sem, (dx, flip) in enumerate(order):
            ref = wide_ref.at[wide_id(dx, flip, 1), :, quarter_lanes(q)]
            described(ref, sib_send.at[sem, q], sib_recv.at[sem, q], sib).wait_recv()

    def multiply(q, part):
        start = quarter_start(z, yl, q)

        def body(t, carry):
            i, j = 2 * part + t // 2, t % 2
            rows, cols = spot(i, j)
            value = tile(wide_ref, narrow_ref, start, i, j)
            if q:
                value = value + sum_ref[rows, cols]
            sum_ref[rows, cols] = value
            return carry

        lax.fori_loop(0, 4, body, 0)

    near_send_group(0, NEAR, (4, 5, 7), 0)
    near_send_group(0, FAR, (4, 5, 6, 7), 2)
    near_send_group(0, NEAR, (1, 2, 3, 6), 1)
    near_send_group(0, FAR, (1, 2, 3), 3)
    own(0)
    near_send_group(0, 1, (1, 2, 3, 4, 5, 6, 7), 4)
    own(1)
    neighbours(0)
    partner(0)
    own(2)
    near_arrive(4, FAR, 2)
    near_send_group(FAR, NEAR, (4 ^ NEAR, 5 ^ NEAR, 6 ^ NEAR, 7 ^ NEAR), 5)
    near_arrive(3, NEAR, 0)
    near_send_group(NEAR, FAR, (4 ^ FAR, 5 ^ FAR, 7 ^ FAR), 6)
    neighbours(1)
    opposite(0)
    partner_neighbours(0)
    own(3)
    partner_opposite(0)
    opposite(1)
    near_arrive(4, NEAR, 1)
    neighbours(2)
    shared(0)
    local[0].wait()
    local[1].wait()
    multiply(0, 0)
    multiply(0, 1)
    near_arrive(7, 1, 4)
    near_send_group(1, NEAR, (1, 4, 5, 7), 7)
    near_send_group(1, FAR, (4, 6, 7), 9)
    near_send_group(1, NEAR, (2, 3, 6), 8)
    near_send_group(1, FAR, (1, 2, 3, 5), 10)
    multiply(0, 2)
    multiply(0, 3)
    partner(1)
    neighbours(3)
    near_arrive(3, FAR, 3)
    near_arrive(4, OPPOSITE, 5)
    near_arrive(3, OPPOSITE, 6)
    partner_neighbours(1)
    partner(2)
    partner_opposite(1)
    shared(1)
    local[2].wait()
    multiply(1, 0)
    near_arrive(3, FAR + 1, 9)
    near_send_group(FAR + 1, NEAR, (4 ^ NEAR, 6 ^ NEAR, 7 ^ NEAR), 11)
    near_arrive(4, NEAR + 1, 7)
    near_send_group(NEAR + 1, FAR, (1 ^ FAR, 4 ^ FAR, 5 ^ FAR, 7 ^ FAR), 12)
    multiply(1, 1)
    partner(3)
    multiply(1, 2)
    partner_neighbours(2)
    multiply(1, 3)
    opposite(2)
    opposite(3)
    partner_opposite(2)
    near_arrive(3, NEAR + 1, 8)
    shared(2)
    local[3].wait()
    multiply(2, 0)
    partner_neighbours(3)
    multiply(2, 1)
    multiply(2, 2)
    multiply(2, 3)
    partner_opposite(3)
    near_arrive(4, FAR + 1, 10)
    near_arrive(3, OPPOSITE + 1, 11)
    near_arrive(4, OPPOSITE + 1, 12)
    shared(3)
    local[4].wait()
    for copy in sent:
        copy.wait_send()
    for count, source, sem, receiver in groups:
        ref = narrow_ref.at[pl.ds(0, count), :, slice_lanes(source)]
        described(ref, near_send.at[sem], near_recv.at[sem], at_narrow(receiver)).wait_send()


def finish_kernel(wide_ref, narrow_ref, sum_ref, out_ref, stage, sems):
    n = lax.axis_index("narrow")
    start = quarter_start(n // 2, n % 2, 3)

    def copy(i, slot):
        rows, _ = spot(i, 0)
        return pltpu.make_async_copy(stage.at[slot], out_ref.at[rows, :], sems.at[slot])

    def body(t, carry):
        for slot in range(2):
            i = 2 * t + slot

            @pl.when(t > 0)
            def _():
                copy(i - 2, slot).wait()

            for j in range(2):
                rows, cols = spot(i, j)
                value = tile(wide_ref, narrow_ref, start, i, j) + sum_ref[rows, cols]
                stage[slot, :, j * COLS:(j + 1) * COLS] = value * (1.0 / SNPS)
            copy(i, slot).start()
        return carry

    steps = WIDE // 4
    lax.fori_loop(0, steps, body, 0)
    for slot in range(2):
        copy(2 * steps - 2 + slot, slot).wait()


def product(own):
    dma = pltpu.SemaphoreType.DMA
    vmem = pl.BlockSpec(memory_space=pltpu.VMEM)
    wide, narrow, total = pl.pallas_call(
        gather_kernel,
        out_shape=(
            pltpu.VMEM((WIDE, SUB, SNPS), jnp.bfloat16),
            pltpu.VMEM((NARROW, SUB, SNPS), jnp.bfloat16),
            pltpu.VMEM((WIDE * SUB, BLK), jnp.float32),
        ),
        in_specs=[vmem],
        out_specs=(vmem, vmem, vmem),
        scratch_shapes=[
            dma((7,)), dma((7,)), dma((6,)),
            dma((9, 4)), dma((9, 4)), dma((8, 4)), dma((8, 4)), dma((13,)), dma((13,)),
        ],
        compiler_params=pltpu.CompilerParams(collective_id=0, has_side_effects=True, vmem_limit_bytes=12 * 1024 * 1024),
    )(own)
    return pl.pallas_call(
        finish_kernel,
        out_shape=jax.ShapeDtypeStruct((WIDE * SUB, BLK), jnp.float32),
        in_specs=[vmem, vmem, vmem],
        out_specs=pl.BlockSpec(memory_space=pl.ANY),
        scratch_shapes=[pltpu.VMEM((2, ROWS, BLK), jnp.float32), dma((2,))],
        compiler_params=pltpu.CompilerParams(vmem_limit_bytes=12 * 1024 * 1024),
    )(wide, narrow, total)


def shards(dosages, allele_counts, called_counts):
    standard = standardize(dosages, allele_counts, called_counts)
    own = standard.T.reshape(NARROW, SUB, PIECE)
    return product(own).reshape(WIDE, 1, SUB, BLK)


def solution(mesh):
    return jax.shard_map(
        shards,
        mesh=mesh,
        in_specs=(P("narrow", "wide"), P("narrow"), P("narrow")),
        out_specs=P(None, "narrow", None, "wide"),
        check_vma=False,
    )
```

```python
import jax
import jax.numpy as jnp
from jax import lax
from jax.experimental import pallas as pl
from jax.experimental.pallas import tpu as pltpu
from jax.sharding import PartitionSpec as P

MESH = pl.DeviceIdType.MESH
SNPS = 2048
SUB = 192
NARROW = 8
WIDE = 16
BLK = NARROW * SUB
PIECE = SNPS // NARROW
QUARTER = SNPS // 4
PARTS = 4
SLOTS = 4
ROWS = WIDE // PARTS * SUB
NEAR, OPPOSITE, FAR = 2, 4, 6


def standardize(dosages, allele_counts, called_counts):
    freq = allele_counts.astype(jnp.float32) / (2.0 * called_counts.astype(jnp.float32))
    freq = freq[:, None]
    values = (dosages.astype(jnp.float32) - 2.0 * freq) * lax.rsqrt(2.0 * freq * (1.0 - freq))
    values = jnp.where(dosages == 3, jnp.zeros_like(values), values)
    return values.astype(jnp.bfloat16)


def quarter_start(z, yl, q):
    half = z // 2
    return (yl if q < 2 else 1 - yl) * (SNPS // 2) + (half if q % 2 == 0 else 1 - half) * QUARTER


def tile(wide_ref, narrow_ref, start, panels):
    lanes = pl.ds(pl.multiple_of(start, QUARTER), QUARTER)
    rows = wide_ref[panels, :, lanes]
    rows = rows.reshape(rows.shape[0] * SUB, QUARTER)
    cols = narrow_ref[:, :, lanes].reshape(BLK, QUARTER)
    return lax.dot_general(rows, cols, (((1,), (1,)), ((), ())), preferred_element_type=jnp.float32)


def gather_kernel(
    own_ref, wide_ref, narrow_ref, sum_ref,
    a2a_send, a2a_recv, local_sem, far_send, far_recv, sib_send, sib_recv, near_send, near_recv,
):
    w, n = lax.axis_index("wide"), lax.axis_index("narrow")
    x, yh, c = w // 4, (w // 2) % 2, w % 2
    z, yl = n // 2, n % 2

    def wide_id(dx, flip, core):
        return ((x + dx) % 4) * 4 + (1 - yh if flip else yh) * 2 + (1 - c if core else c)

    def ring(a):
        return (z, z + 1 - 2 * (z % 2), (z + 2) % 4, 3 - z)[a]

    def side(b):
        return 1 - yl if b else yl

    def narrow_id(label):
        return 2 * ring(label // 2) + side(label % 2)

    def at_wide(dx, flip, core):
        return {"wide": wide_id(dx, flip, core), "narrow": n}

    def at_narrow(label):
        return {"wide": w, "narrow": narrow_id(label)}

    xp, xm, yhp, sib = at_wide(1, 0, 0), at_wide(3, 0, 0), at_wide(0, 1, 0), at_wide(0, 0, 1)
    targets = [at_narrow(label) for label in range(1, NARROW)] + [xp, xm, yhp, sib]
    barrier = pltpu.get_barrier_semaphore()
    for t in targets:
        pl.semaphore_signal(barrier, inc=1, device_id=t, device_id_type=MESH)
    pl.semaphore_wait(barrier, len(targets))

    def slice_lanes(label):
        start = side(label % 2) * (SNPS // 2) + ring(label // 2) * PIECE
        return pl.ds(pl.multiple_of(start, PIECE), PIECE)

    def quarter_lanes(q, half=None):
        if q == 0 and half is not None:
            return slice_lanes(NEAR if half else 0)
        start = quarter_start(z, yl, q)
        if half is None:
            return pl.ds(pl.multiple_of(start, QUARTER), QUARTER)
        return pl.ds(pl.multiple_of(start + half * PIECE, PIECE), PIECE)

    sent = []

    def send(src, dst, ssem, rsem, device, keep=True):
        copy = pltpu.make_async_remote_copy(
            src_ref=src, dst_ref=dst, send_sem=ssem, recv_sem=rsem, device_id=device, device_id_type=MESH
        )
        copy.start()
        if keep:
            sent.append(copy)

    def described(ref, ssem, rsem, device):
        return pltpu.make_async_remote_copy(
            src_ref=ref, dst_ref=ref, send_sem=ssem, recv_sem=rsem, device_id=device, device_id_type=MESH
        )

    def a2a(label):
        send(
            own_ref.at[narrow_id(label)], wide_ref.at[w, :, slice_lanes(0)],
            a2a_send.at[label - 1], a2a_recv.at[label - 1], at_narrow(label),
        )

    own_piece = pltpu.make_async_copy(own_ref.at[n], wide_ref.at[w, :, slice_lanes(0)], local_sem.at[4])
    own_piece.start()
    own_slice = pltpu.make_async_copy(own_ref, narrow_ref.at[:, :, slice_lanes(0)], local_sem.at[5])
    own_slice.start()
    local = [own_slice, own_piece]
    groups = {}

    def near_send_group(source, receiver, labels, sem):
        for i in labels:
            piece = receiver ^ i
            k = narrow_id(piece)
            lanes = slice_lanes(source)
            if source == 0:
                src = own_ref.at[k]
            elif piece == 0:
                src = wide_ref.at[w, :, lanes]
            else:
                src = narrow_ref.at[k, :, lanes]
            send(src, narrow_ref.at[k, :, lanes], near_send.at[sem], near_recv.at[sem], at_narrow(receiver), keep=False)
        groups[sem] = (groups.get(sem, (0,))[0] + len(labels), source, receiver)

    def near_arrive(count, source, sem):
        ref = narrow_ref.at[pl.ds(0, count), :, slice_lanes(source)]
        described(ref, near_send.at[sem], near_recv.at[sem], at_narrow(1)).wait_recv()

    def wide_send(dx, flip, q, sem, device, half=None):
        ref = wide_ref.at[wide_id(dx, flip, 0), :, quarter_lanes(q, half)]
        send(ref, ref, far_send.at[sem, q], far_recv.at[sem, q], device)

    def wide_arrive(dx, flip, q, sem, half=None):
        ref = wide_ref.at[wide_id(dx, flip, 0), :, quarter_lanes(q, half)]
        described(ref, far_send.at[sem, q], far_recv.at[sem, q], yhp).wait_recv()

    def share(dx, flip, q, sem, half=None):
        ref = wide_ref.at[wide_id(dx, flip, 0), :, quarter_lanes(q, half)]
        send(ref, ref, sib_send.at[sem, q], sib_recv.at[sem, q], sib)

    def first_half():
        src, dst = own_ref.at[n], wide_ref.at[w, :, quarter_lanes(0, 0)]
        for sem, device in ((9, xp), (10, xm), (11, yhp)):
            send(src, dst, far_send.at[sem, 0], far_recv.at[sem, 0], device)
        send(src, dst, sib_send.at[8, 0], sib_recv.at[8, 0], sib)

    def own(q):
        labels = ((NEAR,), (FAR, OPPOSITE), (1, NEAR + 1), (FAR + 1, OPPOSITE + 1))[q]
        for label in labels:
            ref = wide_ref.at[w, :, slice_lanes(label)]
            described(ref, a2a_send.at[label - 1], a2a_recv.at[label - 1], at_narrow(1)).wait_recv()
        half = None if q else 1
        wide_send(0, 0, q, 0, xp, half)
        wide_send(0, 0, q, 1, xm, half)
        if q == 0:
            to_partner(0)
        share(0, 0, q, 0, half)
        lanes = quarter_lanes(q, half)
        copy = pltpu.make_async_copy(wide_ref.at[w, :, lanes], narrow_ref.at[n, :, lanes], local_sem.at[q])
        copy.start()
        local.append(copy)

    def to_partner(q):
        wide_send(0, 0, q, 2, yhp, None if q else 1)

    def neighbours(q):
        if q == 0:
            wide_arrive(3, 0, 0, 9, half=0)
            wide_send(3, 0, 0, 5, xp, half=0)
            wide_arrive(1, 0, 0, 10, half=0)
            wide_arrive(1, 0, 0, 1, half=1)
            wide_send(1, 0, 0, 6, xm, half=1)
            wide_arrive(3, 0, 0, 0, half=1)
        else:
            wide_arrive(3, 0, q, 0)
            wide_send(3, 0, q, 5, xp, half=0)
            wide_arrive(1, 0, q, 1)
            wide_send(1, 0, q, 6, xm, half=1)
        share(3, 0, q, 1)
        share(1, 0, q, 2)

    def opposite(q):
        wide_arrive(2, 0, q, 5, half=0)
        wide_arrive(2, 0, q, 6, half=1)
        share(2, 0, q, 3)

    def partner(q):
        if q == 0:
            wide_arrive(0, 1, 0, 11, half=0)
        wide_arrive(0, 1, q, 2, None if q else 1)
        wide_send(0, 1, q, 3, xp, half=0)
        wide_send(0, 1, q, 4, xm, half=1)
        wide_send(0, 1, q, 12, xp, half=1)
        wide_send(0, 1, q, 13, xm, half=0)
        share(0, 1, q, 4)

    def partner_neighbours(q):
        wide_arrive(3, 1, q, 3, half=0)
        wide_send(3, 1, q, 7, xp, half=0)
        wide_arrive(1, 1, q, 4, half=1)
        wide_send(1, 1, q, 8, xm, half=1)

    def partner_opposite(q):
        wide_arrive(3, 1, q, 12, half=1)
        share(3, 1, q, 5)
        wide_arrive(1, 1, q, 13, half=0)
        share(1, 1, q, 6)
        wide_arrive(2, 1, q, 7, half=0)
        wide_arrive(2, 1, q, 8, half=1)
        share(2, 1, q, 7)

    def shared(q):
        order = ((0, 0), (3, 0), (1, 0), (2, 0), (0, 1), (3, 1), (1, 1), (2, 1))
        for sem, (dx, flip) in enumerate(order + ((0, 0),) * (q == 0)):
            half = {0: 1, 8: 0}.get(sem) if q == 0 else None
            ref = wide_ref.at[wide_id(dx, flip, 1), :, quarter_lanes(q, half)]
            described(ref, sib_send.at[sem, q], sib_recv.at[sem, q], sib).wait_recv()

    def multiply(q, part):
        start = quarter_start(z, yl, q)

        def body(p, carry):
            rows = pl.ds(pl.multiple_of(p * ROWS, ROWS), ROWS)
            value = tile(wide_ref, narrow_ref, start, pl.ds(p * (WIDE // PARTS), WIDE // PARTS))
            if q:
                value = value + sum_ref[rows, :]
            sum_ref[rows, :] = value
            return carry

        first = part + n // NARROW
        lax.fori_loop(first, first + 1, body, 0)

    a2a(NEAR)
    a2a(FAR)
    a2a(OPPOSITE)
    a2a(1)
    first_half()
    near_send_group(0, NEAR, (4, 5, 7), 0)
    near_send_group(0, FAR, (4, 5, 6, 7), 2)
    own(0)
    a2a(NEAR + 1)
    a2a(FAR + 1)
    a2a(OPPOSITE + 1)
    near_send_group(0, NEAR, (1, 2, 3, 6), 1)
    near_send_group(0, FAR, (1, 2, 3), 3)
    own(1)
    to_partner(1)
    neighbours(0)
    partner(0)
    near_send_group(0, 1, (4, 5, 6, 7), 4)
    near_send_group(0, 1, (1, 2, 3), 13)
    neighbours(1)
    opposite(0)
    partner_neighbours(0)
    own(2)
    near_arrive(4, FAR, 2)
    near_send_group(FAR, NEAR, (4 ^ NEAR, 5 ^ NEAR, 6 ^ NEAR, 7 ^ NEAR), 5)
    near_arrive(3, NEAR, 0)
    near_send_group(NEAR, FAR, (4 ^ FAR, 5 ^ FAR, 7 ^ FAR), 6)
    partner(1)
    near_arrive(4, 1, 4)
    near_send_group(1, NEAR, (4, 5, 7), 7)
    near_send_group(1, FAR, (1, 2, 3), 10)
    near_send_group(1, NEAR, (2, 6), 8)
    to_partner(2)
    partner_opposite(0)
    near_arrive(4, NEAR, 1)
    shared(0)
    local[0].wait()
    local[1].wait()
    local[2].wait()
    multiply(0, 0)
    multiply(0, 1)
    multiply(0, 2)
    neighbours(2)
    multiply(0, 3)
    partner_neighbours(1)
    own(3)
    to_partner(3)
    near_arrive(3, 1, 13)
    near_send_group(1, NEAR, (1,), 7)
    near_send_group(1, FAR, (4, 6, 7), 9)
    near_send_group(1, NEAR, (3,), 8)
    near_send_group(1, FAR, (5,), 10)
    opposite(1)
    partner(2)
    partner_opposite(1)
    near_arrive(3, FAR, 3)
    near_arrive(4, OPPOSITE, 5)
    near_arrive(3, OPPOSITE, 6)
    shared(1)
    local[3].wait()
    multiply(1, 0)
    multiply(1, 1)
    multiply(1, 2)
    neighbours(3)
    multiply(1, 3)
    partner_neighbours(2)
    partner(3)
    near_arrive(3, FAR + 1, 9)
    near_send_group(FAR + 1, NEAR, (4 ^ NEAR, 6 ^ NEAR, 7 ^ NEAR), 11)
    near_arrive(4, NEAR + 1, 7)
    near_send_group(NEAR + 1, FAR, (1 ^ FAR, 4 ^ FAR, 5 ^ FAR, 7 ^ FAR), 12)
    opposite(2)
    opposite(3)
    partner_opposite(2)
    near_arrive(3, NEAR + 1, 8)
    shared(2)
    local[4].wait()
    multiply(2, 0)
    partner_neighbours(3)
    multiply(2, 1)
    multiply(2, 2)
    multiply(2, 3)
    partner_opposite(3)
    near_arrive(4, FAR + 1, 10)
    near_arrive(3, OPPOSITE + 1, 11)
    near_arrive(4, OPPOSITE + 1, 12)
    shared(3)
    local[5].wait()
    for copy in sent:
        copy.wait_send()
    for sem, (count, source, receiver) in groups.items():
        ref = narrow_ref.at[pl.ds(0, count), :, slice_lanes(source)]
        described(ref, near_send.at[sem], near_recv.at[sem], at_narrow(receiver)).wait_send()


def finish_kernel(wide_ref, narrow_ref, sum_ref, out_ref, stage, sems):
    n = lax.axis_index("narrow")
    start = quarter_start(n // 2, n % 2, 3)
    copies = []
    panel = 0
    for i, count in enumerate((1, 1, 2, 2, 2, 2, 2, 2, 2)):
        slot, rows = i % SLOTS, slice(panel * SUB, (panel + count) * SUB)
        if i >= SLOTS:
            copies[i - SLOTS].wait()
        value = tile(wide_ref, narrow_ref, start, pl.ds(panel, count)) + sum_ref[rows, :]
        stage[slot, : count * SUB, :] = value * (1.0 / SNPS)
        copy = pltpu.make_async_copy(stage.at[slot, : count * SUB, :], out_ref.at[rows, :], sems.at[slot])
        copy.start()
        copies.append(copy)
        panel += count
    for copy in copies[-SLOTS:]:
        copy.wait()


def product(own):
    dma = pltpu.SemaphoreType.DMA
    vmem = pl.BlockSpec(memory_space=pltpu.VMEM)
    wide, narrow, total = pl.pallas_call(
        gather_kernel,
        out_shape=(
            pltpu.VMEM((WIDE, SUB, SNPS), jnp.bfloat16),
            pltpu.VMEM((NARROW, SUB, SNPS), jnp.bfloat16),
            pltpu.VMEM((WIDE * SUB, BLK), jnp.float32),
        ),
        in_specs=[vmem],
        out_specs=(vmem, vmem, vmem),
        scratch_shapes=[
            dma((7,)), dma((7,)), dma((6,)),
            dma((14, 4)), dma((14, 4)), dma((9, 4)), dma((9, 4)), dma((14,)), dma((14,)),
        ],
        compiler_params=pltpu.CompilerParams(collective_id=0, has_side_effects=True, vmem_limit_bytes=10 * 1024 * 1024),
    )(own)
    return pl.pallas_call(
        finish_kernel,
        out_shape=jax.ShapeDtypeStruct((WIDE * SUB, BLK), jnp.float32),
        in_specs=[vmem, vmem, vmem],
        out_specs=pl.BlockSpec(memory_space=pl.ANY),
        scratch_shapes=[pltpu.VMEM((SLOTS, 2 * SUB, BLK), jnp.float32), dma((SLOTS,))],
        compiler_params=pltpu.CompilerParams(vmem_limit_bytes=14 * 1024 * 1024),
    )(wide, narrow, total)


def shards(dosages, allele_counts, called_counts):
    standard = standardize(dosages, allele_counts, called_counts)
    own = standard.T.reshape(NARROW, SUB, PIECE)
    return product(own).reshape(WIDE, 1, SUB, BLK)


def solution(mesh):
    return jax.shard_map(
        shards,
        mesh=mesh,
        in_specs=(P("narrow", "wide"), P("narrow"), P("narrow")),
        out_specs=P(None, "narrow", None, "wide"),
        check_vma=False,
    )
```

```python
import jax
import jax.numpy as jnp
from jax import lax
from jax.experimental import pallas as pl
from jax.experimental.pallas import tpu as pltpu
from jax.sharding import PartitionSpec as P

MESH = pl.DeviceIdType.MESH
SNPS = 2048
SUB = 192
NARROW = 8
WIDE = 16
BLK = NARROW * SUB
PIECE = SNPS // NARROW
QUARTER = SNPS // 4
PARTS = 4
SLOTS = 4
ROWS = WIDE // PARTS * SUB
NEAR, OPPOSITE, FAR = 2, 4, 6


def standardize_kernel(dosages_ref, allele_hbm, called_hbm, out_ref, blocks, allele_ref, called_ref, sems):
    width = 2 * SUB
    counts = []
    for k, (src, dst) in enumerate(((allele_hbm, allele_ref), (called_hbm, called_ref))):
        copy = pltpu.make_async_copy(src, dst, sems.at[4 + k])
        copy.start()
        counts.append(copy)
    copies = []
    for k in range(BLK // width):
        copy = pltpu.make_async_copy(dosages_ref.at[:, k * width:(k + 1) * width], blocks.at[k], sems.at[k])
        copy.start()
        copies.append(copy)
    for copy in counts:
        copy.wait()
    freq = allele_ref[...].astype(jnp.float32) / (2.0 * called_ref[...].astype(jnp.float32))
    scale = lax.rsqrt(2.0 * freq * (1.0 - freq))
    for k, copy in enumerate(copies):
        copy.wait()
        dosages = blocks[k].astype(jnp.float32).T
        values = jnp.where(dosages == 3.0, 0.0, (dosages - 2.0 * freq) * scale)
        out_ref[2 * k:2 * k + 2] = values.astype(jnp.bfloat16).reshape(2, SUB, PIECE)


def hbm(array):
    return pltpu.with_memory_space_constraint(array, pltpu.HBM)


def standardize(dosages, allele_counts, called_counts):
    vmem = pl.BlockSpec(memory_space=pltpu.VMEM)
    return pl.pallas_call(
        standardize_kernel,
        out_shape=pltpu.VMEM((NARROW, SUB, PIECE), jnp.bfloat16),
        in_specs=[pl.BlockSpec(memory_space=pltpu.HBM)] * 3,
        out_specs=vmem,
        scratch_shapes=[
            pltpu.VMEM((4, PIECE, 2 * SUB), jnp.int32),
            pltpu.VMEM((1, PIECE), jnp.int32),
            pltpu.VMEM((1, PIECE), jnp.int32),
            pltpu.SemaphoreType.DMA((6,)),
        ],
        compiler_params=pltpu.CompilerParams(vmem_limit_bytes=8 * 1024 * 1024),
    )(hbm(dosages), hbm(allele_counts.reshape(1, PIECE)), hbm(called_counts.reshape(1, PIECE)))


def quarter_start(z, yl, q):
    half = z // 2
    return (yl if q < 2 else 1 - yl) * (SNPS // 2) + (half if q % 2 == 0 else 1 - half) * QUARTER


def tile(wide_ref, narrow_ref, start, panels):
    lanes = pl.ds(pl.multiple_of(start, QUARTER), QUARTER)
    rows = wide_ref[panels, :, lanes]
    rows = rows.reshape(rows.shape[0] * SUB, QUARTER)
    cols = narrow_ref[:, :, lanes].reshape(BLK, QUARTER)
    return lax.dot_general(rows, cols, (((1,), (1,)), ((), ())), preferred_element_type=jnp.float32)


def gather_kernel(
    own_ref, wide_ref, narrow_ref, sum_ref,
    a2a_recv, local_sem, far_send, far_recv, sib_send, sib_recv, near_send, near_recv,
):
    w, n = lax.axis_index("wide"), lax.axis_index("narrow")
    x, yh, c = w // 4, (w // 2) % 2, w % 2
    z, yl = n // 2, n % 2

    def wide_id(dx, flip, core):
        return ((x + dx) % 4) * 4 + (1 - yh if flip else yh) * 2 + (1 - c if core else c)

    def ring(a):
        return (z, z + 1 - 2 * (z % 2), (z + 2) % 4, 3 - z)[a]

    def side(b):
        return 1 - yl if b else yl

    def narrow_id(label):
        return 2 * ring(label // 2) + side(label % 2)

    def at_wide(dx, flip, core):
        return {"wide": wide_id(dx, flip, core), "narrow": n}

    def at_narrow(label):
        return {"wide": w, "narrow": narrow_id(label)}

    xp, xm, yhp, sib = at_wide(1, 0, 0), at_wide(3, 0, 0), at_wide(0, 1, 0), at_wide(0, 0, 1)
    targets = [at_narrow(label) for label in range(1, NARROW)] + [xp, xm, yhp, sib]
    barrier = pltpu.get_barrier_semaphore()
    for t in targets:
        pl.semaphore_signal(barrier, inc=1, device_id=t, device_id_type=MESH)
    pl.semaphore_wait(barrier, len(targets))

    def slice_lanes(label):
        start = side(label % 2) * (SNPS // 2) + ring(label // 2) * PIECE
        return pl.ds(pl.multiple_of(start, PIECE), PIECE)

    def quarter_lanes(q, half=None):
        if q == 0 and half is not None:
            return slice_lanes(NEAR if half else 0)
        start = quarter_start(z, yl, q)
        if half is None:
            return pl.ds(pl.multiple_of(start, QUARTER), QUARTER)
        return pl.ds(pl.multiple_of(start + half * PIECE, PIECE), PIECE)

    def send(src, dst, ssem, rsem, device):
        pltpu.make_async_remote_copy(
            src_ref=src, dst_ref=dst, send_sem=ssem, recv_sem=rsem, device_id=device, device_id_type=MESH
        ).start()

    def described(ref, ssem, rsem, device):
        return pltpu.make_async_remote_copy(
            src_ref=ref, dst_ref=ref, send_sem=ssem, recv_sem=rsem, device_id=device, device_id_type=MESH
        )

    def a2a(label):
        send(
            own_ref.at[narrow_id(label)], wide_ref.at[w, :, slice_lanes(0)],
            near_send, a2a_recv.at[label - 1], at_narrow(label),
        )

    own_piece = pltpu.make_async_copy(own_ref.at[n], wide_ref.at[w, :, slice_lanes(0)], local_sem.at[4])
    own_piece.start()
    own_slice = pltpu.make_async_copy(own_ref, narrow_ref.at[:, :, slice_lanes(0)], local_sem.at[5])
    own_slice.start()
    local = [own_slice, own_piece]

    def near_send_group(source, receiver, labels, sem):
        for i in labels:
            piece = receiver ^ i
            k = narrow_id(piece)
            lanes = slice_lanes(source)
            if source == 0:
                src = own_ref.at[k]
            elif piece == 0:
                src = wide_ref.at[w, :, lanes]
            else:
                src = narrow_ref.at[k, :, lanes]
            send(src, narrow_ref.at[k, :, lanes], near_send, near_recv.at[sem], at_narrow(receiver))

    def near_arrive(count, source, sem):
        ref = narrow_ref.at[pl.ds(0, count), :, slice_lanes(source)]
        described(ref, near_send, near_recv.at[sem], at_narrow(1)).wait_recv()

    def wide_send(dx, flip, q, sem, device, half=None):
        ref = wide_ref.at[wide_id(dx, flip, 0), :, quarter_lanes(q, half)]
        send(ref, ref, far_send, far_recv.at[sem, q], device)

    def wide_arrive(dx, flip, q, sem, half=None):
        ref = wide_ref.at[wide_id(dx, flip, 0), :, quarter_lanes(q, half)]
        described(ref, far_send, far_recv.at[sem, q], yhp).wait_recv()

    def share(dx, flip, q, half=None):
        ref = wide_ref.at[wide_id(dx, flip, 0), :, quarter_lanes(q, half)]
        send(ref, ref, sib_send, sib_recv.at[q], sib)

    def first_half():
        src, dst = own_ref.at[n], wide_ref.at[w, :, quarter_lanes(0, 0)]
        for sem, device in ((9, xp), (10, xm), (11, yhp)):
            send(src, dst, far_send, far_recv.at[sem, 0], device)
        send(src, dst, sib_send, sib_recv.at[0], sib)

    def ready(q):
        labels = ((NEAR,), (FAR, OPPOSITE), (1, NEAR + 1), (FAR + 1, OPPOSITE + 1))[q]
        for label in labels:
            ref = wide_ref.at[w, :, slice_lanes(label)]
            described(ref, near_send, a2a_recv.at[label - 1], at_narrow(1)).wait_recv()
        lanes = quarter_lanes(q, None if q else 1)
        copy = pltpu.make_async_copy(wide_ref.at[w, :, lanes], narrow_ref.at[n, :, lanes], local_sem.at[q])
        copy.start()
        local.append(copy)

    def own(q):
        half = None if q else 1
        wide_send(0, 0, q, 0, xp, half)
        wide_send(0, 0, q, 1, xm, half)
        share(0, 0, q, half)

    def to_partner(q):
        wide_send(0, 0, q, 2, yhp, None if q else 1)

    def neighbours(q):
        if q == 0:
            wide_arrive(3, 0, 0, 9, half=0)
            wide_send(3, 0, 0, 5, xp, half=0)
            wide_arrive(1, 0, 0, 10, half=0)
            wide_arrive(1, 0, 0, 1, half=1)
            wide_send(1, 0, 0, 6, xm, half=1)
            wide_arrive(3, 0, 0, 0, half=1)
        else:
            wide_arrive(3, 0, q, 0)
            wide_send(3, 0, q, 5, xp, half=0)
            wide_arrive(1, 0, q, 1)
            wide_send(1, 0, q, 6, xm, half=1)
        share(3, 0, q)
        share(1, 0, q)

    def opposite(q):
        wide_arrive(2, 0, q, 5, half=0)
        wide_arrive(2, 0, q, 6, half=1)
        share(2, 0, q)

    def opposite_to_partner(q):
        wide_send(2, 0, q, 7, yhp)

    def partner_first():
        wide_arrive(0, 1, 0, 11, half=0)
        wide_send(0, 1, 0, 3, xp, half=0)
        wide_send(0, 1, 0, 13, xm, half=0)

    def partner(q):
        wide_arrive(0, 1, q, 2, None if q else 1)
        if q:
            wide_send(0, 1, q, 3, xp, half=0)
        wide_send(0, 1, q, 4, xm, half=1)
        wide_send(0, 1, q, 12, xp, half=1)
        if q:
            wide_send(0, 1, q, 13, xm, half=0)
        share(0, 1, q)

    def partner_neighbours(q):
        if q == 2:
            wide_arrive(3, 1, q, 3, half=0)
            wide_arrive(1, 1, q, 4, half=1)
            return
        wide_arrive(3, 1, q, 3, half=0)
        wide_send(3, 1, q, 7, xp, half=0)
        wide_arrive(1, 1, q, 4, half=1)
        wide_send(1, 1, q, 8, xm, half=1)

    def partner_opposite(q):
        wide_arrive(3, 1, q, 12, half=1)
        share(3, 1, q)
        wide_arrive(1, 1, q, 13, half=0)
        share(1, 1, q)
        if q == 2:
            wide_arrive(2, 1, q, 7)
        else:
            wide_arrive(2, 1, q, 7, half=0)
            wide_arrive(2, 1, q, 8, half=1)
        share(2, 1, q)

    def shared(q):
        ref = wide_ref.at[pl.ds(0, WIDE // 2), :, quarter_lanes(q)]
        described(ref, sib_send, sib_recv.at[q], sib).wait_recv()

    def multiply(q, part):
        start = quarter_start(z, yl, q)

        def body(p, carry):
            rows = pl.ds(pl.multiple_of(p * ROWS, ROWS), ROWS)
            value = tile(wide_ref, narrow_ref, start, pl.ds(p * (WIDE // PARTS), WIDE // PARTS))
            if q:
                value = value + sum_ref[rows, :]
            sum_ref[rows, :] = value
            return carry

        first = part + n // NARROW
        lax.fori_loop(first, first + 1, body, 0)

    a2a(NEAR)
    a2a(FAR)
    first_half()
    a2a(OPPOSITE)
    a2a(1)
    near_send_group(0, NEAR, (4, 5, 7), 0)
    near_send_group(0, FAR, (4, 5, 6, 7), 2)
    ready(0)
    own(0)
    to_partner(0)
    partner_first()
    a2a(NEAR + 1)
    a2a(FAR + 1)
    a2a(OPPOSITE + 1)
    near_send_group(0, NEAR, (1, 2, 3, 6), 1)
    near_send_group(0, FAR, (1, 2, 3), 3)
    ready(1)
    own(1)
    to_partner(1)
    neighbours(0)
    partner(0)
    near_send_group(0, 1, (2, 5, 6, 7), 4)
    neighbours(1)
    ready(2)
    to_partner(2)
    near_send_group(0, 1, (1, 3, 4), 13)
    opposite(0)
    partner_neighbours(0)
    own(2)
    near_arrive(4, FAR, 2)
    near_send_group(FAR, NEAR, (4 ^ NEAR, 5 ^ NEAR, 6 ^ NEAR, 7 ^ NEAR), 5)
    near_arrive(3, NEAR, 0)
    near_send_group(NEAR, FAR, (4 ^ FAR, 5 ^ FAR, 7 ^ FAR), 6)
    partner(1)
    partner_opposite(0)
    near_arrive(4, NEAR, 1)
    shared(0)
    local[0].wait()
    local[1].wait()
    local[2].wait()
    multiply(0, 0)
    multiply(0, 1)
    near_arrive(4, 1, 4)
    near_send_group(1, NEAR, (7, 4), 7)
    near_send_group(1, FAR, (4, 6), 9)
    near_send_group(1, NEAR, (5, 2), 8)
    near_send_group(1, FAR, (3, 1), 10)
    multiply(0, 2)
    neighbours(2)
    multiply(0, 3)
    partner_neighbours(1)
    ready(3)
    own(3)
    to_partner(3)
    opposite(1)
    partner_opposite(1)
    near_arrive(3, FAR, 3)
    near_arrive(4, OPPOSITE, 5)
    near_arrive(3, OPPOSITE, 6)
    shared(1)
    local[3].wait()
    multiply(1, 0)
    near_arrive(3, 1, 13)
    near_send_group(1, NEAR, (3, 1, 6), 8)
    near_send_group(1, FAR, (7, 5, 2), 10)
    partner(2)
    opposite(2)
    opposite_to_partner(2)
    multiply(1, 1)
    multiply(1, 2)
    partner(3)
    neighbours(3)
    multiply(1, 3)
    near_arrive(2, FAR + 1, 9)
    near_send_group(FAR + 1, NEAR, (4 ^ NEAR, 6 ^ NEAR), 11)
    near_arrive(2, NEAR + 1, 7)
    near_send_group(NEAR + 1, FAR, (4 ^ FAR, 7 ^ FAR), 12)
    near_send_group(OPPOSITE, 1, (3, 5, 7), 14)
    partner_neighbours(2)
    partner_neighbours(3)
    partner_opposite(2)
    near_arrive(5, NEAR + 1, 8)
    shared(2)
    local[4].wait()
    multiply(2, 0)
    opposite(3)
    multiply(2, 1)
    multiply(2, 2)
    partner_opposite(3)
    multiply(2, 3)
    near_arrive(5, FAR + 1, 10)
    near_arrive(2, OPPOSITE + 1, 11)
    near_arrive(2, OPPOSITE + 1, 12)
    near_arrive(3, OPPOSITE + 1, 14)
    shared(3)
    local[5].wait()
    for panels, sem in ((7, far_send), (8, sib_send), (7, near_send)):
        described(wide_ref.at[pl.ds(0, panels)], sem, sem, sib).wait_send()


def finish_kernel(wide_ref, narrow_ref, sum_ref, out_ref, stage, sems):
    n = lax.axis_index("narrow")
    start = quarter_start(n // 2, n % 2, 3)
    copies = []
    panel = 0
    for i, count in enumerate((1, 1, 2, 2, 2, 2, 2, 2, 2)):
        slot, rows = i % SLOTS, slice(panel * SUB, (panel + count) * SUB)
        if i >= SLOTS:
            copies[i - SLOTS].wait()
        value = tile(wide_ref, narrow_ref, start, pl.ds(panel, count)) + sum_ref[rows, :]
        stage[slot, : count * SUB, :] = value * (1.0 / SNPS)
        copy = pltpu.make_async_copy(stage.at[slot, : count * SUB, :], out_ref.at[rows, :], sems.at[slot])
        copy.start()
        copies.append(copy)
        panel += count
    for copy in copies[-SLOTS:]:
        copy.wait()


def product(own):
    dma = pltpu.SemaphoreType.DMA
    vmem = pl.BlockSpec(memory_space=pltpu.VMEM)
    wide, narrow, total = pl.pallas_call(
        gather_kernel,
        out_shape=(
            pltpu.VMEM((WIDE, SUB, SNPS), jnp.bfloat16),
            pltpu.VMEM((NARROW, SUB, SNPS), jnp.bfloat16),
            pltpu.VMEM((WIDE * SUB, BLK), jnp.float32),
        ),
        in_specs=[vmem],
        out_specs=(vmem, vmem, vmem),
        scratch_shapes=[
            dma((7,)), dma((6,)), dma(()), dma((14, 4)), dma(()), dma((4,)), dma(()), dma((15,)),
        ],
        compiler_params=pltpu.CompilerParams(collective_id=0, has_side_effects=True, vmem_limit_bytes=10 * 1024 * 1024),
    )(own)
    return pl.pallas_call(
        finish_kernel,
        out_shape=jax.ShapeDtypeStruct((WIDE * SUB, BLK), jnp.float32),
        in_specs=[vmem, vmem, vmem],
        out_specs=pl.BlockSpec(memory_space=pl.ANY),
        scratch_shapes=[pltpu.VMEM((SLOTS, 2 * SUB, BLK), jnp.float32), dma((SLOTS,))],
        compiler_params=pltpu.CompilerParams(vmem_limit_bytes=14 * 1024 * 1024),
    )(wide, narrow, total)


def shards(dosages, allele_counts, called_counts):
    own = standardize(dosages, allele_counts, called_counts)
    return product(own).reshape(WIDE, 1, SUB, BLK)


def solution(mesh):
    return jax.shard_map(
        shards,
        mesh=mesh,
        in_specs=(P("narrow", "wide"), P("narrow"), P("narrow")),
        out_specs=P(None, "narrow", None, "wide"),
        check_vma=False,
    )
```

```python
import jax
import jax.numpy as jnp
from jax import lax
from jax.experimental import pallas as pl
from jax.experimental.pallas import tpu as pltpu
from jax.sharding import PartitionSpec as P

MESH = pl.DeviceIdType.MESH
SNPS = 2048
SUB = 192
NARROW = 8
WIDE = 16
BLK = NARROW * SUB
PIECE = SNPS // NARROW
QUARTER = SNPS // 4
PARTS = 4
SLOTS = 4
ROWS = WIDE // PARTS * SUB
NEAR, OPPOSITE, FAR = 2, 4, 6
ARRIVAL = {NEAR: 0, FAR: 1, OPPOSITE: 1, 1: 2, NEAR + 1: 2, FAR + 1: 3, OPPOSITE + 1: 3}


def standardize_kernel(dosages_ref, allele_hbm, called_hbm, out_ref, blocks, allele_ref, called_ref, sems):
    width = 2 * SUB
    counts = []
    for k, (src, dst) in enumerate(((allele_hbm, allele_ref), (called_hbm, called_ref))):
        copy = pltpu.make_async_copy(src, dst, sems.at[4 + k])
        copy.start()
        counts.append(copy)
    copies = []
    for k in range(BLK // width):
        copy = pltpu.make_async_copy(dosages_ref.at[:, k * width:(k + 1) * width], blocks.at[k], sems.at[k])
        copy.start()
        copies.append(copy)
    for copy in counts:
        copy.wait()
    freq = allele_ref[...].astype(jnp.float32) / (2.0 * called_ref[...].astype(jnp.float32))
    scale = lax.rsqrt(2.0 * freq * (1.0 - freq))
    for k, copy in enumerate(copies):
        copy.wait()
        dosages = blocks[k].astype(jnp.float32).T
        values = jnp.where(dosages == 3.0, 0.0, (dosages - 2.0 * freq) * scale)
        out_ref[2 * k:2 * k + 2] = values.astype(jnp.bfloat16).reshape(2, SUB, PIECE)


def hbm(array):
    return pltpu.with_memory_space_constraint(array, pltpu.HBM)


def standardize(dosages, allele_counts, called_counts):
    vmem = pl.BlockSpec(memory_space=pltpu.VMEM)
    return pl.pallas_call(
        standardize_kernel,
        out_shape=pltpu.VMEM((NARROW, SUB, PIECE), jnp.bfloat16),
        in_specs=[pl.BlockSpec(memory_space=pltpu.HBM)] * 3,
        out_specs=vmem,
        scratch_shapes=[
            pltpu.VMEM((4, PIECE, 2 * SUB), jnp.int32),
            pltpu.VMEM((1, PIECE), jnp.int32),
            pltpu.VMEM((1, PIECE), jnp.int32),
            pltpu.SemaphoreType.DMA((6,)),
        ],
        compiler_params=pltpu.CompilerParams(vmem_limit_bytes=8 * 1024 * 1024),
    )(hbm(dosages), hbm(allele_counts.reshape(1, PIECE)), hbm(called_counts.reshape(1, PIECE)))


def quarter_start(z, yl, q):
    half = z // 2
    return (yl if q < 2 else 1 - yl) * (SNPS // 2) + (half if q % 2 == 0 else 1 - half) * QUARTER


def tile(wide_ref, narrow_ref, start, panels):
    lanes = pl.ds(pl.multiple_of(start, QUARTER), QUARTER)
    rows = wide_ref[panels, :, lanes]
    rows = rows.reshape(rows.shape[0] * SUB, QUARTER)
    cols = narrow_ref[:, :, lanes].reshape(BLK, QUARTER)
    return lax.dot_general(rows, cols, (((1,), (1,)), ((), ())), preferred_element_type=jnp.float32)


def gather_kernel(
    own_ref, wide_ref, narrow_ref, sum_ref,
    a2a_recv, local_sem, far_send, far_recv, sib_send, sib_recv, near_send, near_recv,
):
    w, n = lax.axis_index("wide"), lax.axis_index("narrow")
    x, yh, c = w // 4, (w // 2) % 2, w % 2
    z, yl = n // 2, n % 2

    def wide_id(dx, flip, core):
        return ((x + dx) % 4) * 4 + (1 - yh if flip else yh) * 2 + (1 - c if core else c)

    def ring(a):
        return (z, z + 1 - 2 * (z % 2), (z + 2) % 4, 3 - z)[a]

    def side(b):
        return 1 - yl if b else yl

    def narrow_id(label):
        return 2 * ring(label // 2) + side(label % 2)

    def at_wide(dx, flip, core):
        return {"wide": wide_id(dx, flip, core), "narrow": n}

    def at_narrow(label):
        return {"wide": w, "narrow": narrow_id(label)}

    xp, xm, yhp, sib = at_wide(1, 0, 0), at_wide(3, 0, 0), at_wide(0, 1, 0), at_wide(0, 0, 1)
    targets = [at_narrow(label) for label in range(1, NARROW)] + [xp, xm, yhp, sib]
    barrier = pltpu.get_barrier_semaphore()
    for t in targets:
        pl.semaphore_signal(barrier, inc=1, device_id=t, device_id_type=MESH)
    pl.semaphore_wait(barrier, len(targets))

    def slice_lanes(label):
        start = side(label % 2) * (SNPS // 2) + ring(label // 2) * PIECE
        return pl.ds(pl.multiple_of(start, PIECE), PIECE)

    def quarter_lanes(q, half=None):
        if q == 0 and half is not None:
            return slice_lanes(NEAR if half else 0)
        start = quarter_start(z, yl, q)
        if half is None:
            return pl.ds(pl.multiple_of(start, QUARTER), QUARTER)
        return pl.ds(pl.multiple_of(start + half * PIECE, PIECE), PIECE)

    def send(src, dst, ssem, rsem, device):
        pltpu.make_async_remote_copy(
            src_ref=src, dst_ref=dst, send_sem=ssem, recv_sem=rsem, device_id=device, device_id_type=MESH
        ).start()

    def described(ref, ssem, rsem):
        return pltpu.make_async_remote_copy(
            src_ref=ref, dst_ref=ref, send_sem=ssem, recv_sem=rsem, device_id=sib, device_id_type=MESH
        )

    def a2a(label):
        send(
            own_ref.at[narrow_id(label)], wide_ref.at[w, :, slice_lanes(0)],
            near_send, a2a_recv.at[ARRIVAL[label]], at_narrow(label),
        )

    own_piece = pltpu.make_async_copy(own_ref.at[n], wide_ref.at[w, :, slice_lanes(0)], local_sem.at[4])
    own_piece.start()
    own_slice = pltpu.make_async_copy(own_ref, narrow_ref.at[:, :, slice_lanes(0)], local_sem.at[5])
    own_slice.start()
    local = [own_slice, own_piece]

    def near_send_group(source, receiver, labels, sem):
        for i in labels:
            piece = receiver ^ i
            k = narrow_id(piece)
            lanes = slice_lanes(source)
            if source == 0:
                src = own_ref.at[k]
            elif piece == 0:
                src = wide_ref.at[w, :, lanes]
            else:
                src = narrow_ref.at[k, :, lanes]
            send(src, narrow_ref.at[k, :, lanes], near_send, near_recv.at[sem], at_narrow(receiver))

    def near_arrive(count, source, sem):
        ref = wide_ref.at[pl.ds(0, count), :, slice_lanes(source)]
        described(ref, near_send, near_recv.at[sem]).wait_recv()

    def far(sem, q):
        return 32 + sem - 9 if 9 <= sem <= 11 else {6: 5, 7: 6, 8: 6, 12: 7, 13: 7}.get(sem, sem) * 4 + q

    def wide_send(dx, flip, q, sem, device, half=None):
        ref = wide_ref.at[wide_id(dx, flip, 0), :, quarter_lanes(q, half)]
        send(ref, ref, far_send, far_recv.at[far(sem, q)], device)

    def wide_arrive(dx, flip, q, sem, half=None):
        ref = wide_ref.at[wide_id(dx, flip, 0), :, quarter_lanes(q, half)]
        described(ref, far_send, far_recv.at[far(sem, q)]).wait_recv()

    def share(dx, flip, q, half=None):
        ref = wide_ref.at[wide_id(dx, flip, 0), :, quarter_lanes(q, half)]
        send(ref, ref, sib_send, sib_recv.at[q], sib)

    def first_half():
        src, dst = own_ref.at[n], wide_ref.at[w, :, quarter_lanes(0, 0)]
        for sem, device in ((9, xp), (10, xm), (11, yhp)):
            send(src, dst, far_send, far_recv.at[far(sem, 0)], device)
        send(src, dst, sib_send, sib_recv.at[0], sib)

    def ready(q):
        lanes = quarter_lanes(q, None if q else 1)
        ref = wide_ref.at[w, :, lanes]
        described(ref, near_send, a2a_recv.at[q]).wait_recv()
        copy = pltpu.make_async_copy(wide_ref.at[w, :, lanes], narrow_ref.at[n, :, lanes], local_sem.at[q])
        copy.start()
        local.append(copy)

    def own(q):
        half = None if q else 1
        wide_send(0, 0, q, 0, xp, half)
        wide_send(0, 0, q, 1, xm, half)
        share(0, 0, q, half)

    def to_partner(q):
        wide_send(0, 0, q, 2, yhp, None if q else 1)

    def neighbours(q):
        if q == 0:
            wide_arrive(3, 0, 0, 9, half=0)
            wide_send(3, 0, 0, 5, xp, half=0)
            wide_arrive(1, 0, 0, 10, half=0)
            wide_arrive(1, 0, 0, 1, half=1)
            wide_send(1, 0, 0, 6, xm, half=1)
            wide_arrive(3, 0, 0, 0, half=1)
        else:
            wide_arrive(3, 0, q, 0)
            wide_send(3, 0, q, 5, xp, half=0)
            wide_arrive(1, 0, q, 1)
            wide_send(1, 0, q, 6, xm, half=1)
        share(3, 0, q)
        share(1, 0, q)

    def opposite(q):
        wide_arrive(2, 0, q, 5)
        share(2, 0, q)

    def opposite_to_partner(q):
        wide_send(2, 0, q, 7, yhp)

    def partner_first():
        wide_arrive(0, 1, 0, 11, half=0)
        wide_send(0, 1, 0, 3, xp, half=0)
        wide_send(0, 1, 0, 13, xm, half=0)

    def partner(q):
        wide_arrive(0, 1, q, 2, None if q else 1)
        if q:
            wide_send(0, 1, q, 3, xp, half=0)
        wide_send(0, 1, q, 4, xm, half=1)
        wide_send(0, 1, q, 12, xp, half=1)
        if q:
            wide_send(0, 1, q, 13, xm, half=0)
        share(0, 1, q)

    def partner_neighbours(q):
        if q == 2:
            wide_arrive(3, 1, q, 3, half=0)
            wide_arrive(1, 1, q, 4, half=1)
            return
        wide_arrive(3, 1, q, 3, half=0)
        wide_send(3, 1, q, 7, xp, half=0)
        wide_arrive(1, 1, q, 4, half=1)
        wide_send(1, 1, q, 8, xm, half=1)

    def partner_opposite(q):
        wide_arrive(3, 1, q, 12)
        share(3, 1, q)
        share(1, 1, q)
        wide_arrive(2, 1, q, 7)
        share(2, 1, q)

    def shared(q):
        ref = wide_ref.at[pl.ds(0, WIDE // 2), :, quarter_lanes(q)]
        described(ref, sib_send, sib_recv.at[q]).wait_recv()

    def multiply(q, part):
        start = quarter_start(z, yl, q)

        def body(p, carry):
            rows = pl.ds(pl.multiple_of(p * ROWS, ROWS), ROWS)
            value = tile(wide_ref, narrow_ref, start, pl.ds(p * (WIDE // PARTS), WIDE // PARTS))
            if q:
                value = value + sum_ref[rows, :]
            sum_ref[rows, :] = value
            return carry

        first = part + n // NARROW
        lax.fori_loop(first, first + 1, body, 0)

    a2a(NEAR)
    a2a(FAR)
    first_half()
    a2a(OPPOSITE)
    a2a(1)
    near_send_group(0, NEAR, (1, 4, 5, 7), 0)
    near_send_group(0, FAR, (4, 6, 7), 2)
    ready(0)
    own(0)
    to_partner(0)
    partner_first()
    a2a(NEAR + 1)
    a2a(FAR + 1)
    a2a(OPPOSITE + 1)
    ready(1)
    own(1)
    to_partner(1)
    near_send_group(0, NEAR, (2, 3, 6), 1)
    near_send_group(0, FAR, (1, 2, 3, 5), 3)
    neighbours(0)
    partner(0)
    near_send_group(0, 1, (2, 5, 6, 7), 4)
    neighbours(1)
    ready(2)
    to_partner(2)
    near_send_group(0, 1, (1, 3, 4), 5)
    opposite(0)
    partner_neighbours(0)
    own(2)
    near_arrive(3, FAR, 2)
    near_send_group(FAR, NEAR, (4 ^ NEAR, 6 ^ NEAR, 7 ^ NEAR), 3)
    near_arrive(4, NEAR, 0)
    near_send_group(NEAR, FAR, (1 ^ FAR, 4 ^ FAR, 5 ^ FAR, 7 ^ FAR), 3)
    partner(1)
    partner_opposite(0)
    near_arrive(3, NEAR, 1)
    shared(0)
    local[0].wait()
    local[1].wait()
    local[2].wait()
    multiply(0, 0)
    multiply(0, 1)
    near_arrive(4, 1, 4)
    near_send_group(1, NEAR, (7, 4), 6)
    near_send_group(1, FAR, (4, 6), 8)
    near_send_group(1, NEAR, (5, 2), 7)
    near_send_group(1, FAR, (3, 1), 9)
    multiply(0, 2)
    neighbours(2)
    multiply(0, 3)
    partner_neighbours(1)
    ready(3)
    own(3)
    to_partner(3)
    opposite(1)
    partner_opposite(1)
    near_arrive(11, FAR, 3)
    shared(1)
    local[3].wait()
    multiply(1, 0)
    near_arrive(3, 1, 5)
    near_send_group(1, NEAR, (3, 1, 6), 7)
    near_send_group(1, FAR, (7, 5, 2), 9)
    partner(2)
    opposite(2)
    opposite_to_partner(2)
    multiply(1, 1)
    multiply(1, 2)
    partner(3)
    neighbours(3)
    multiply(1, 3)
    near_arrive(2, FAR + 1, 8)
    near_send_group(FAR + 1, NEAR, (4 ^ NEAR, 6 ^ NEAR), 9)
    near_arrive(2, NEAR + 1, 6)
    near_send_group(NEAR + 1, FAR, (4 ^ FAR, 7 ^ FAR), 9)
    near_send_group(OPPOSITE, 1, (3, 5, 7), 9)
    partner_neighbours(2)
    partner_opposite(2)
    near_arrive(5, NEAR + 1, 7)
    shared(2)
    local[4].wait()
    multiply(2, 0)
    partner_neighbours(3)
    multiply(2, 1)
    multiply(2, 2)
    opposite(3)
    partner_opposite(3)
    multiply(2, 3)
    near_arrive(12, FAR + 1, 9)
    shared(3)
    local[5].wait()
    for panels, sem in ((7, far_send), (8, sib_send), (7, near_send)):
        described(wide_ref.at[pl.ds(0, panels)], sem, sem).wait_send()


def finish_kernel(wide_ref, narrow_ref, sum_ref, out_ref, stage, sems):
    n = lax.axis_index("narrow")
    start = quarter_start(n // 2, n % 2, 3)
    copies = []
    panel = 0
    for i, count in enumerate((2,) * (WIDE // 2)):
        slot, rows = i % SLOTS, slice(panel * SUB, (panel + count) * SUB)
        if i >= SLOTS:
            copies[i - SLOTS].wait()
        value = tile(wide_ref, narrow_ref, start, pl.ds(panel, count)) + sum_ref[rows, :]
        stage[slot, : count * SUB, :] = value * (1.0 / SNPS)
        copy = pltpu.make_async_copy(stage.at[slot, : count * SUB, :], out_ref.at[rows, :], sems.at[slot])
        copy.start()
        copies.append(copy)
        panel += count
    for copy in copies[-SLOTS:]:
        copy.wait()


def product(own):
    dma = pltpu.SemaphoreType.DMA
    vmem = pl.BlockSpec(memory_space=pltpu.VMEM)
    wide, narrow, total = pl.pallas_call(
        gather_kernel,
        out_shape=(
            pltpu.VMEM((WIDE, SUB, SNPS), jnp.bfloat16),
            pltpu.VMEM((NARROW, SUB, SNPS), jnp.bfloat16),
            pltpu.VMEM((WIDE * SUB, BLK), jnp.float32),
        ),
        in_specs=[vmem],
        out_specs=(vmem, vmem, vmem),
        scratch_shapes=[
            dma((4,)), dma((6,)), dma(()), dma((35,)), dma(()), dma((4,)), dma(()), dma((10,)),
        ],
        compiler_params=pltpu.CompilerParams(collective_id=0, has_side_effects=True, vmem_limit_bytes=10 * 1024 * 1024),
    )(own)
    return pl.pallas_call(
        finish_kernel,
        out_shape=jax.ShapeDtypeStruct((WIDE * SUB, BLK), jnp.float32),
        in_specs=[vmem, vmem, vmem],
        out_specs=pl.BlockSpec(memory_space=pl.ANY),
        scratch_shapes=[pltpu.VMEM((SLOTS, 2 * SUB, BLK), jnp.float32), dma((SLOTS,))],
        compiler_params=pltpu.CompilerParams(vmem_limit_bytes=14 * 1024 * 1024),
    )(wide, narrow, total)


def shards(dosages, allele_counts, called_counts):
    own = standardize(dosages, allele_counts, called_counts)
    return product(own).reshape(WIDE, 1, SUB, BLK)


def solution(mesh):
    return jax.shard_map(
        shards,
        mesh=mesh,
        in_specs=(P("narrow", "wide"), P("narrow"), P("narrow")),
        out_specs=P(None, "narrow", None, "wide"),
        check_vma=False,
    )
```

```python
import jax
import jax.numpy as jnp
from jax import lax
from jax.experimental import pallas as pl
from jax.experimental.pallas import tpu as pltpu
from jax.sharding import PartitionSpec as P

MESH = pl.DeviceIdType.MESH
SNPS = 2048
SUB = 192
NARROW = 8
WIDE = 16
BLK = NARROW * SUB
PIECE = SNPS // NARROW
QUARTER = SNPS // 4
PARTS = 4
SLOTS = 4
ROWS = WIDE // PARTS * SUB
NEAR, OPPOSITE, FAR = 2, 4, 6
ARRIVAL = {NEAR: 0, FAR: 1, OPPOSITE: 1, 1: 2, NEAR + 1: 2, FAR + 1: 3, OPPOSITE + 1: 3}


def standardize_kernel(dosages_ref, allele_hbm, called_hbm, out_ref, blocks, allele_ref, called_ref, sems):
    width = 2 * SUB
    counts = []
    for k, (src, dst) in enumerate(((allele_hbm, allele_ref), (called_hbm, called_ref))):
        copy = pltpu.make_async_copy(src, dst, sems.at[4 + k])
        copy.start()
        counts.append(copy)
    copies = []
    for k in range(BLK // width):
        copy = pltpu.make_async_copy(dosages_ref.at[:, k * width:(k + 1) * width], blocks.at[k], sems.at[k])
        copy.start()
        copies.append(copy)
    for copy in counts:
        copy.wait()
    freq = allele_ref[...].astype(jnp.float32) / (2.0 * called_ref[...].astype(jnp.float32))
    scale = lax.rsqrt(2.0 * freq * (1.0 - freq))
    for k, copy in enumerate(copies):
        copy.wait()
        dosages = blocks[k].astype(jnp.float32).T
        values = jnp.where(dosages == 3.0, 0.0, (dosages - 2.0 * freq) * scale)
        out_ref[2 * k:2 * k + 2] = values.astype(jnp.bfloat16).reshape(2, SUB, PIECE)


def hbm(array):
    return pltpu.with_memory_space_constraint(array, pltpu.HBM)


def standardize(dosages, allele_counts, called_counts):
    vmem = pl.BlockSpec(memory_space=pltpu.VMEM)
    return pl.pallas_call(
        standardize_kernel,
        out_shape=pltpu.VMEM((NARROW, SUB, PIECE), jnp.bfloat16),
        in_specs=[pl.BlockSpec(memory_space=pltpu.HBM)] * 3,
        out_specs=vmem,
        scratch_shapes=[
            pltpu.VMEM((4, PIECE, 2 * SUB), jnp.int32),
            pltpu.VMEM((1, PIECE), jnp.int32),
            pltpu.VMEM((1, PIECE), jnp.int32),
            pltpu.SemaphoreType.DMA((6,)),
        ],
        compiler_params=pltpu.CompilerParams(vmem_limit_bytes=8 * 1024 * 1024),
    )(hbm(dosages), hbm(allele_counts.reshape(1, PIECE)), hbm(called_counts.reshape(1, PIECE)))


def quarter_start(z, yl, q):
    half = z // 2
    return (yl if q < 2 else 1 - yl) * (SNPS // 2) + (half if q % 2 == 0 else 1 - half) * QUARTER


def tile(wide_ref, narrow_ref, start, panels):
    lanes = pl.ds(pl.multiple_of(start, QUARTER), QUARTER)
    rows = wide_ref[panels, :, lanes]
    rows = rows.reshape(rows.shape[0] * SUB, QUARTER)
    cols = narrow_ref[:, :, lanes].reshape(BLK, QUARTER)
    return lax.dot_general(rows, cols, (((1,), (1,)), ((), ())), preferred_element_type=jnp.float32)


def gather_kernel(
    own_ref, wide_ref, narrow_ref, sum_ref,
    a2a_recv, local_sem, far_send, far_recv, sib_send, sib_recv, near_send, near_recv,
):
    w, n = lax.axis_index("wide"), lax.axis_index("narrow")
    x, yh, c = w // 4, (w // 2) % 2, w % 2
    z, yl = n // 2, n % 2

    def wide_id(dx, flip, core):
        return ((x + dx) % 4) * 4 + (1 - yh if flip else yh) * 2 + (1 - c if core else c)

    def ring(a):
        return (z, z + 1 - 2 * (z % 2), (z + 2) % 4, 3 - z)[a]

    def side(b):
        return 1 - yl if b else yl

    def narrow_id(label):
        return 2 * ring(label // 2) + side(label % 2)

    def at_wide(dx, flip, core):
        return {"wide": wide_id(dx, flip, core), "narrow": n}

    def at_narrow(label):
        return {"wide": w, "narrow": narrow_id(label)}

    xp, xm, yhp, sib = at_wide(1, 0, 0), at_wide(3, 0, 0), at_wide(0, 1, 0), at_wide(0, 0, 1)
    targets = [at_narrow(label) for label in range(1, NARROW)] + [xp, xm, yhp, sib]
    barrier = pltpu.get_barrier_semaphore()
    for t in targets:
        pl.semaphore_signal(barrier, inc=1, device_id=t, device_id_type=MESH)
    pl.semaphore_wait(barrier, len(targets))

    def slice_lanes(label):
        start = side(label % 2) * (SNPS // 2) + ring(label // 2) * PIECE
        return pl.ds(pl.multiple_of(start, PIECE), PIECE)

    def quarter_lanes(q, half=None):
        if q == 0 and half is not None:
            return slice_lanes(NEAR if half else 0)
        start = quarter_start(z, yl, q)
        if half is None:
            return pl.ds(pl.multiple_of(start, QUARTER), QUARTER)
        return pl.ds(pl.multiple_of(start + half * PIECE, PIECE), PIECE)

    def send(src, dst, ssem, rsem, device):
        pltpu.make_async_remote_copy(
            src_ref=src, dst_ref=dst, send_sem=ssem, recv_sem=rsem, device_id=device, device_id_type=MESH
        ).start()

    def described(ref, ssem, rsem):
        return pltpu.make_async_remote_copy(
            src_ref=ref, dst_ref=ref, send_sem=ssem, recv_sem=rsem, device_id=sib, device_id_type=MESH
        )

    def a2a(label):
        send(
            own_ref.at[narrow_id(label)], wide_ref.at[w, :, slice_lanes(0)],
            near_send, a2a_recv.at[ARRIVAL[label]], at_narrow(label),
        )

    own_piece = pltpu.make_async_copy(own_ref.at[n], wide_ref.at[w, :, slice_lanes(0)], local_sem.at[4])
    own_piece.start()
    own_slice = pltpu.make_async_copy(own_ref, narrow_ref.at[:, :, slice_lanes(0)], local_sem.at[5])
    own_slice.start()
    local = [own_slice, own_piece]

    def near_send_group(source, receiver, labels, sem):
        for i in labels:
            piece = receiver ^ i
            k = narrow_id(piece)
            lanes = slice_lanes(source)
            if source == 0:
                src = own_ref.at[k]
            elif piece == 0:
                src = wide_ref.at[w, :, lanes]
            else:
                src = narrow_ref.at[k, :, lanes]
            send(src, narrow_ref.at[k, :, lanes], near_send, near_recv.at[sem], at_narrow(receiver))

    def near_arrive(count, source, sem):
        ref = wide_ref.at[pl.ds(0, count), :, slice_lanes(source)]
        described(ref, near_send, near_recv.at[sem]).wait_recv()

    def far(sem, q):
        return 32 + sem - 9 if 9 <= sem <= 11 else {6: 5, 7: 6, 8: 6, 12: 7, 13: 7}.get(sem, sem) * 4 + q

    def wide_send(dx, flip, q, sem, device, half=None):
        ref = wide_ref.at[wide_id(dx, flip, 0), :, quarter_lanes(q, half)]
        send(ref, ref, far_send, far_recv.at[far(sem, q)], device)

    def wide_arrive(dx, flip, q, sem, half=None):
        ref = wide_ref.at[wide_id(dx, flip, 0), :, quarter_lanes(q, half)]
        described(ref, far_send, far_recv.at[far(sem, q)]).wait_recv()

    def share(dx, flip, q, half=None):
        ref = wide_ref.at[wide_id(dx, flip, 0), :, quarter_lanes(q, half)]
        send(ref, ref, sib_send, sib_recv.at[q], sib)

    def first_half():
        src, dst = own_ref.at[n], wide_ref.at[w, :, quarter_lanes(0, 0)]
        for sem, device in ((9, xp), (10, xm), (11, yhp)):
            send(src, dst, far_send, far_recv.at[far(sem, 0)], device)
        send(src, dst, sib_send, sib_recv.at[0], sib)

    def ready(q):
        lanes = quarter_lanes(q, None if q else 1)
        ref = wide_ref.at[w, :, lanes]
        described(ref, near_send, a2a_recv.at[q]).wait_recv()
        copy = pltpu.make_async_copy(wide_ref.at[w, :, lanes], narrow_ref.at[n, :, lanes], local_sem.at[q])
        copy.start()
        local.append(copy)

    def own(q):
        half = None if q else 1
        wide_send(0, 0, q, 0, xp, half)
        wide_send(0, 0, q, 1, xm, half)
        share(0, 0, q, half)

    def to_partner(q):
        wide_send(0, 0, q, 2, yhp, None if q else 1)

    def neighbours(q):
        if q == 0:
            wide_arrive(3, 0, 0, 9, half=0)
            wide_send(3, 0, 0, 5, xp, half=0)
            wide_arrive(1, 0, 0, 10, half=0)
            wide_arrive(1, 0, 0, 1, half=1)
            wide_send(1, 0, 0, 6, xm, half=1)
            wide_arrive(3, 0, 0, 0, half=1)
        else:
            wide_arrive(3, 0, q, 0)
            wide_send(3, 0, q, 5, xp, half=0)
            wide_arrive(1, 0, q, 1)
            wide_send(1, 0, q, 6, xm, half=1)
        share(3, 0, q)
        share(1, 0, q)

    def opposite(q):
        wide_arrive(2, 0, q, 5)
        share(2, 0, q)

    def opposite_to_partner(q):
        wide_send(2, 0, q, 7, yhp)

    def partner_first():
        wide_arrive(0, 1, 0, 11, half=0)
        wide_send(0, 1, 0, 3, xp, half=0)
        wide_send(0, 1, 0, 13, xm, half=0)

    def partner(q):
        wide_arrive(0, 1, q, 2, None if q else 1)
        if q:
            wide_send(0, 1, q, 3, xp, half=0)
        wide_send(0, 1, q, 4, xm, half=1)
        wide_send(0, 1, q, 12, xp, half=1)
        if q:
            wide_send(0, 1, q, 13, xm, half=0)
        share(0, 1, q)

    def partner_neighbours(q):
        if q == 2:
            wide_arrive(3, 1, q, 3, half=0)
            wide_arrive(1, 1, q, 4, half=1)
            return
        wide_arrive(3, 1, q, 3, half=0)
        wide_send(3, 1, q, 7, xp, half=0)
        wide_arrive(1, 1, q, 4, half=1)
        wide_send(1, 1, q, 8, xm, half=1)

    def partner_opposite(q):
        wide_arrive(3, 1, q, 12)
        share(3, 1, q)
        share(1, 1, q)
        wide_arrive(2, 1, q, 7)
        share(2, 1, q)

    def shared(q):
        ref = wide_ref.at[pl.ds(0, WIDE // 2), :, quarter_lanes(q)]
        described(ref, sib_send, sib_recv.at[q]).wait_recv()

    def multiply(q, part):
        start = quarter_start(z, yl, q)

        def body(p, carry):
            rows = pl.ds(pl.multiple_of(p * ROWS, ROWS), ROWS)
            value = tile(wide_ref, narrow_ref, start, pl.ds(p * (WIDE // PARTS), WIDE // PARTS))
            if q:
                value = value + sum_ref[rows, :]
            sum_ref[rows, :] = value
            return carry

        first = part + n // NARROW
        lax.fori_loop(first, first + 1, body, 0)

    a2a(NEAR)
    a2a(FAR)
    first_half()
    a2a(OPPOSITE)
    a2a(1)
    near_send_group(0, NEAR, (1, 4, 5, 7), 0)
    near_send_group(0, FAR, (4, 6, 7), 2)
    ready(0)
    own(0)
    to_partner(0)
    partner_first()
    a2a(NEAR + 1)
    a2a(FAR + 1)
    a2a(OPPOSITE + 1)
    ready(1)
    own(1)
    to_partner(1)
    near_send_group(0, NEAR, (2, 3, 6), 1)
    near_send_group(0, FAR, (1, 2, 3, 5), 3)
    neighbours(0)
    partner(0)
    near_send_group(0, 1, (2, 5, 6, 7), 4)
    neighbours(1)
    ready(2)
    to_partner(2)
    near_send_group(0, 1, (1, 3, 4), 5)
    opposite(0)
    partner_neighbours(0)
    own(2)
    near_arrive(3, FAR, 2)
    near_send_group(FAR, NEAR, (4 ^ NEAR, 6 ^ NEAR, 7 ^ NEAR), 3)
    near_arrive(4, NEAR, 0)
    near_send_group(NEAR, FAR, (1 ^ FAR, 4 ^ FAR, 5 ^ FAR, 7 ^ FAR), 3)
    partner(1)
    partner_opposite(0)
    near_arrive(3, NEAR, 1)
    shared(0)
    local[0].wait()
    local[1].wait()
    local[2].wait()
    multiply(0, 0)
    neighbours(2)
    multiply(0, 1)
    near_arrive(4, 1, 4)
    near_send_group(1, NEAR, (7, 4), 6)
    near_send_group(1, FAR, (4, 6), 8)
    near_send_group(1, NEAR, (5, 2), 7)
    near_send_group(1, FAR, (3, 1), 9)
    partner_neighbours(1)
    ready(3)
    own(3)
    to_partner(3)
    multiply(0, 2)
    multiply(0, 3)
    opposite(1)
    partner(2)
    opposite(2)
    partner_opposite(1)
    near_arrive(3, 1, 5)
    near_send_group(1, NEAR, (3, 1, 6), 7)
    near_send_group(1, FAR, (7, 5, 2), 9)
    near_arrive(11, FAR, 3)
    shared(1)
    local[3].wait()
    multiply(1, 0)
    partner(3)
    opposite_to_partner(2)
    multiply(1, 1)
    neighbours(3)
    multiply(1, 2)
    multiply(1, 3)
    near_arrive(2, FAR + 1, 8)
    near_send_group(FAR + 1, NEAR, (4 ^ NEAR, 6 ^ NEAR), 9)
    near_arrive(2, NEAR + 1, 6)
    near_send_group(NEAR + 1, FAR, (4 ^ FAR, 7 ^ FAR), 9)
    near_send_group(OPPOSITE, 1, (3, 5, 7), 9)
    partner_neighbours(2)
    partner_opposite(2)
    near_arrive(5, NEAR + 1, 7)
    shared(2)
    local[4].wait()
    multiply(2, 0)
    partner_neighbours(3)
    multiply(2, 1)
    multiply(2, 2)
    opposite(3)
    partner_opposite(3)
    multiply(2, 3)
    near_arrive(12, FAR + 1, 9)
    shared(3)
    local[5].wait()
    for panels, sem in ((7, far_send), (8, sib_send), (7, near_send)):
        described(wide_ref.at[pl.ds(0, panels)], sem, sem).wait_send()


def finish_kernel(wide_ref, narrow_ref, sum_ref, out_ref, stage, sems):
    n = lax.axis_index("narrow")
    start = quarter_start(n // 2, n % 2, 3)
    copies = []
    panel = 0
    for i, count in enumerate((2,) * (WIDE // 2)):
        slot, rows = i % SLOTS, slice(panel * SUB, (panel + count) * SUB)
        if i >= SLOTS:
            copies[i - SLOTS].wait()
        value = tile(wide_ref, narrow_ref, start, pl.ds(panel, count)) + sum_ref[rows, :]
        stage[slot, : count * SUB, :] = value * (1.0 / SNPS)
        copy = pltpu.make_async_copy(stage.at[slot, : count * SUB, :], out_ref.at[rows, :], sems.at[slot])
        copy.start()
        copies.append(copy)
        panel += count
    for copy in copies[-SLOTS:]:
        copy.wait()


def product(own):
    dma = pltpu.SemaphoreType.DMA
    vmem = pl.BlockSpec(memory_space=pltpu.VMEM)
    wide, narrow, total = pl.pallas_call(
        gather_kernel,
        out_shape=(
            pltpu.VMEM((WIDE, SUB, SNPS), jnp.bfloat16),
            pltpu.VMEM((NARROW, SUB, SNPS), jnp.bfloat16),
            pltpu.VMEM((WIDE * SUB, BLK), jnp.float32),
        ),
        in_specs=[vmem],
        out_specs=(vmem, vmem, vmem),
        scratch_shapes=[
            dma((4,)), dma((6,)), dma(()), dma((35,)), dma(()), dma((4,)), dma(()), dma((10,)),
        ],
        compiler_params=pltpu.CompilerParams(collective_id=0, has_side_effects=True, vmem_limit_bytes=10 * 1024 * 1024),
    )(own)
    return pl.pallas_call(
        finish_kernel,
        out_shape=jax.ShapeDtypeStruct((WIDE * SUB, BLK), jnp.float32),
        in_specs=[vmem, vmem, vmem],
        out_specs=pl.BlockSpec(memory_space=pl.ANY),
        scratch_shapes=[pltpu.VMEM((SLOTS, 2 * SUB, BLK), jnp.float32), dma((SLOTS,))],
        compiler_params=pltpu.CompilerParams(vmem_limit_bytes=14 * 1024 * 1024),
    )(wide, narrow, total)


def shards(dosages, allele_counts, called_counts):
    own = standardize(dosages, allele_counts, called_counts)
    return product(own).reshape(WIDE, 1, SUB, BLK)


def solution(mesh):
    return jax.shard_map(
        shards,
        mesh=mesh,
        in_specs=(P("narrow", "wide"), P("narrow"), P("narrow")),
        out_specs=P(None, "narrow", None, "wide"),
        check_vma=False,
    )
```
